256 devices in a mesh: section: 16 (over z_lo, y), tensor: 16 (over x, z_hi, core).
Axes of the slice: x: 4, y: 4, z: 8 (z_hi: 2, z_lo: 4; z = z_hi * 4 + z_lo), core: 2. Of those that a mesh axis runs over, the one named last changes fastest.
Arguments:
- inputs_down: bfloat16 [16, 224, 8192], P('section', None, 'tensor'), may hold values from -18 to 18
- inputs_up: bfloat16 [16, 224, 8192], P('section', None, 'tensor'), may hold values from -18 to 18
- grads_down: bfloat16 [16, 224, 8192], P('section', None, 'tensor'), may hold values from -6 to 6
- grads_up: bfloat16 [16, 224, 8192], P('section', None, 'tensor'), may hold values from -6 to 6
- weights_down: bfloat16 [16, 8192, 2048], P('section', 'tensor'), may hold values from -0.5 to 0.5
- weights_up: bfloat16 [16, 8192, 2048], P('section', 'tensor'), may hold values from -0.5 to 0.5
Outputs:
- handed_down: bfloat16 [16, 224, 8192], P('section', None, 'tensor')
- handed_up: bfloat16 [16, 224, 8192], P('section', None, 'tensor')
- returned_down: bfloat16 [16, 224, 8192], P('section', None, 'tensor')
- returned_up: bfloat16 [16, 224, 8192], P('section', None, 'tensor')
- weight_grads: float32 [16, 8192, 2048], P('section', 'tensor')
The draws below stay inside these ranges and needn't reach their ends.
All inputs are finite; a program needn't handle non-finite values.
Results may differ from the reference program's by a relative error of at most 0.0095.
Values may be sent and summed in bfloat16 or wider, within the bound.
A program may use at most 64 MiB of HBM per device.

```python
import jax
import jax.numpy as jnp
from jax import lax

D = 8192
HEADS = 64
KV_HEADS = 8
HEAD_DIM = 128
TOKENS = 224
SECTIONS = 16


def draw_field(key, salt):
    keys = jax.random.split(jax.random.fold_in(key, salt), 1)
    shape = (SECTIONS, TOKENS, D)
    columns = 0.6 * jnp.exp(jnp.log(3.0) * jnp.arange(D, dtype=jnp.float32) / D)
    field = jax.random.truncated_normal(keys[0], -5.0, 5.0, shape, jnp.float32) * columns
    return field.astype(jnp.bfloat16)


def draw_matrix(key, salt):
    keys = jax.random.split(jax.random.fold_in(key, salt), 1)
    shape = (SECTIONS, D, 2 * KV_HEADS * HEAD_DIM)
    matrix = jax.random.truncated_normal(keys[0], -4.0, 4.0, shape, jnp.float32) / jnp.sqrt(1.0 * D)
    return matrix.astype(jnp.bfloat16)


def draw_inputs_down(key, part):
    return draw_field(key, 11)


def draw_inputs_up(key, part):
    return draw_field(key, 23)


def draw_weights_down(key, part):
    return draw_matrix(key, 37)


def draw_weights_up(key, part):
    return draw_matrix(key, 41)


def levels(rng, extent, cuts, smallest, high):
    factor_of, own = 1.0, jax.random.fold_in(rng, 6)
    for dim, shards_of in cuts:
        steps = jnp.exp(jax.random.uniform(jax.random.fold_in(own, dim), (shards_of,), jnp.float32, smallest / len(cuts), high / len(cuts)))
        factor_of = factor_of * jnp.repeat(steps, extent[dim] // shards_of).reshape([-1 if axis == dim else 1 for axis in range(len(extent))])
    return factor_of


def centred(key, shape, scale, bound, pieces=(), held_as=jnp.bfloat16):
    entries = jax.random.normal(key, shape, jnp.float32) * scale
    if len(pieces) > 0:
        entries = levels(key, shape, pieces, -0.22, 0.18) * entries
    return jnp.clip(entries, min=-bound, max=bound).astype(held_as)


def setup_inputs(seed: int = 0) -> dict:
    splits = jax.random.split(jax.random.key(seed), 7)
    inputs_down = draw_inputs_down(jax.random.fold_in(splits[6], 71), 0)
    inputs_up = draw_inputs_up(jax.random.fold_in(splits[6], 71), 0)
    grads_down = centred(splits[2], (SECTIONS, TOKENS, D), 1.0, 6.0, ((0, 16), (2, 16)))
    grads_up = centred(splits[3], (SECTIONS, TOKENS, D), 1.0, 6.0, ((0, 16), (2, 16)))
    weights_down = draw_weights_down(jax.random.fold_in(splits[6], 71), 0)
    weights_up = draw_weights_up(jax.random.fold_in(splits[6], 71), 0)
    return dict(inputs_down=inputs_down, inputs_up=inputs_up, grads_down=grads_down, grads_up=grads_up, weights_down=weights_down, weights_up=weights_up)


EPS = 1e-05
NEG_BIG = -1e+30

def section_pass(inputs, grads, weights):
    tokens = inputs.shape[0]
    group = HEADS // KV_HEADS
    kv_width = KV_HEADS * HEAD_DIM
    scale = HEAD_DIM ** (-0.5)
    x_float = inputs.astype(jnp.float32)
    scale_rows = lax.rsqrt(lax.optimization_barrier(jnp.mean(x_float * x_float, axis=1, keepdims=True)) + EPS)
    normed = x_float * scale_rows
    hidden = normed.astype(jnp.bfloat16)
    keyval = jnp.dot(hidden, weights, preferred_element_type=jnp.float32).astype(jnp.bfloat16)
    key_rows = jnp.repeat(keyval[:, :kv_width].reshape(tokens, KV_HEADS, HEAD_DIM), group, axis=1).astype(jnp.float32)
    value_rows = jnp.repeat(keyval[:, kv_width:].reshape(tokens, KV_HEADS, HEAD_DIM), group, axis=1).astype(jnp.float32)
    queries = hidden.reshape(tokens, HEADS, HEAD_DIM).astype(jnp.float32)
    places = jnp.arange(tokens)
    causal = places[:, None] >= places[None, :]
    scores = jnp.einsum('qhd,khd->hqk', queries, key_rows) * scale
    scores = jnp.where(causal[None], scores, NEG_BIG)
    score_peak = lax.optimization_barrier(jnp.max(scores, axis=-1, keepdims=True))
    score_exp = jnp.exp(scores - score_peak)
    attn_probs = score_exp / lax.optimization_barrier(jnp.sum(score_exp, axis=-1, keepdims=True))
    probs_low = lax.optimization_barrier(attn_probs.astype(jnp.bfloat16)).astype(jnp.float32)
    attended = jnp.einsum('hqk,khd->qhd', probs_low, value_rows).reshape(tokens, D)
    output = (x_float + attended).astype(jnp.bfloat16)
    upstream = grads.astype(jnp.float32).reshape(tokens, HEADS, HEAD_DIM)
    grad_prob = jnp.einsum('qhd,khd->hqk', upstream, value_rows)
    grad_value_heads = jnp.einsum('hqk,qhd->khd', probs_low, upstream)
    grad_score = attn_probs * (grad_prob - lax.optimization_barrier(jnp.sum(attn_probs * grad_prob, axis=-1, keepdims=True)))
    grad_score_low = lax.optimization_barrier(grad_score.astype(jnp.bfloat16)).astype(jnp.float32)
    grad_query = jnp.einsum('hqk,khd->qhd', grad_score_low, key_rows) * scale
    grad_key_heads = jnp.einsum('hqk,qhd->khd', grad_score_low, queries) * scale
    grad_keys = grad_key_heads.reshape(tokens, KV_HEADS, group, HEAD_DIM).sum(axis=2).reshape(tokens, kv_width)
    grad_values = grad_value_heads.reshape(tokens, KV_HEADS, group, HEAD_DIM).sum(axis=2).reshape(tokens, kv_width)
    grad_kv = jnp.concatenate([grad_keys, grad_values], axis=1).astype(jnp.bfloat16)
    grad_hidden = grad_query.reshape(tokens, D) + jnp.dot(grad_kv, weights.T, preferred_element_type=jnp.float32)
    inner_mean = lax.optimization_barrier(jnp.mean(grad_hidden * normed, axis=1, keepdims=True))
    grad_input = (grads.astype(jnp.float32) + scale_rows * (grad_hidden - normed * inner_mean)).astype(jnp.bfloat16)
    grad_weights = jnp.dot(hidden.T, grad_kv, preferred_element_type=jnp.float32)
    return (output, grad_input, grad_weights)

def run_copy(inputs, grads, weights):
    return lax.map(lambda items: section_pass(items[0], items[1], items[2]), (inputs, grads, weights))

def reference(inputs_down, inputs_up, grads_down, grads_up, weights_down, weights_up):
    out_down, back_down, dw_down = run_copy(inputs_down, grads_down, weights_down)
    out_up, back_up, dw_up = run_copy(inputs_up, grads_up, weights_up)
    blank = jnp.zeros_like(out_down[:1])
    handed_down = jnp.concatenate([blank, out_down[:-1]], axis=0)
    handed_up = jnp.concatenate([out_up[1:], blank], axis=0)
    returned_down = jnp.concatenate([back_down[1:], blank], axis=0)
    returned_up = jnp.concatenate([blank, back_up[:-1]], axis=0)
    weight_grads = dw_down + jnp.flip(dw_up, axis=0)
    return (handed_down, handed_up, returned_down, returned_up, weight_grads)
```

```python
import jax
import jax.numpy as jnp
from jax import lax
from jax.experimental import pallas as pl
from jax.experimental.pallas import tpu as pltpu
from jax.sharding import PartitionSpec as P

MESH = pl.DeviceIdType.MESH
F32 = jnp.float32
BF16 = jnp.bfloat16

D = 8192
HEAD_DIM = 128
EPS = 1e-05
NEG_BIG = -1e30
SCALE = HEAD_DIM ** (-0.5)

T = 224
W = 512
HALF = 1024
QH = W // HEAD_DIM
LANES = 256

UP, DOWN, MIRROR = 0, 1, 2


def dot(a, b, ca, cb):
    return lax.dot_general(a, b, (((ca,), (cb,)), ((), ())), preferred_element_type=F32)


def row_of(total):
    return jnp.sum(jnp.transpose(total), axis=0, keepdims=True)


def column_of(row):
    return jnp.transpose(jnp.broadcast_to(row, (128, T)))


def exchange_kernel(sections, *refs):
    (xd_h, xu_h, gd_h, gu_h, wd_h, wu_h) = refs[:6]
    (hd_o, hu_o, rd_o, ru_o, hidt_o, gath_o) = refs[6:12]
    (x, g, w, xm, bias, zeros, hidt) = refs[12:19]
    (psend, precv, xsend, xrecv, acc, zsend, zrecv, kvf, kv, rcol) = refs[19:29]
    (dq, dkv, dkvr, gath, out, gin) = refs[29:35]
    (s0, s1, s2, s3, srp, srx, srz, srm) = refs[35:43]
    (i0, i1, i2, irz, irx, irp) = refs[43:49]
    (lsem, ssem, rsem) = refs[49:52]

    sec = lax.axis_index("section")
    t = lax.axis_index("tensor")
    xi, zi, c = t // 4, (t // 2) % 2, t % 2
    mine, other = c * HALF, (1 - c) * HALF
    head = xi * 2 + zi

    def at(x_, z_, c_):
        return (sec, x_ * 4 + z_ * 2 + c_)

    partner = at(xi, zi, 1 - c)
    zpeer = at(xi, 1 - zi, c)
    xpeer = {d: at((xi + d) % 4, zi, c) for d in (1, 2, 3)}
    mirror = (sections - 1 - sec, t)
    after = (lax.rem(sec + 1, sections), t)
    before = (lax.rem(sec + sections - 1, sections), t)
    has_after = sec < sections - 1
    has_before = sec > 0

    used = [0, 0]

    def remote(src, dst, dev):
        n = used[0]
        used[0] += 1
        return pltpu.make_async_remote_copy(
            src_ref=src, dst_ref=dst, send_sem=ssem.at[n], recv_sem=rsem.at[n],
            device_id=dev, device_id_type=MESH)

    def local(src, dst):
        n = used[1]
        used[1] += 1
        return pltpu.make_async_copy(src, dst, lsem.at[n])

    sends = []

    def go(src, dst, dev):
        copy = remote(src, dst, dev)
        copy.start()
        sends.append(copy)
        return copy

    barrier = pltpu.get_barrier_semaphore()
    for dev in (partner, zpeer, xpeer[1], xpeer[2], xpeer[3], mirror):
        pl.semaphore_signal(barrier, inc=1, device_id=dev, device_id_type=MESH)

    @pl.when(has_after)
    def _():
        pl.semaphore_signal(barrier, inc=1, device_id=after, device_id_type=MESH)

    @pl.when(has_before)
    def _():
        pl.semaphore_signal(barrier, inc=1, device_id=before, device_id_type=MESH)

    load_x = [local(xu_h, x.at[UP]), local(xd_h, x.at[DOWN])]
    load_g = [local(gu_h, g.at[UP]), local(gd_h, g.at[DOWN])]
    mcols, ocols = pl.ds(pl.multiple_of(mine, HALF), HALF), pl.ds(pl.multiple_of(other, HALF), HALF)
    wh = (wu_h, wd_h)
    load_wo = [local(wh[k].at[:, ocols], w.at[k, :, ocols]) for k in (UP, DOWN)]
    load_wm = [local(wh[k].at[:, mcols], w.at[k, :, mcols]) for k in (UP, DOWN)]
    load_x[UP].start()
    load_wo[UP].start()
    load_wm[UP].start()
    load_x[DOWN].start()
    load_wo[DOWN].start()
    load_wm[DOWN].start()
    load_g[UP].start()
    load_g[DOWN].start()

    def block(k, base, d):
        col = pl.multiple_of(base + ((xi + d) % 4) * 256, 128)
        return dot(x[k], w[k, :, pl.ds(col, 256)], 1, 0)

    def squares(k):
        v = x[k].astype(F32)
        v = v * v
        total = v[:, 0:128] + v[:, 128:256] + v[:, 256:384] + v[:, 384:512]
        s0[k : k + 1, 0:T] = row_of(total)

    ORDER = (2, 1, 3, 0)

    def for_partner(k, started):
        load_wo[k].wait()
        copies = {}
        for d in ORDER:
            v = block(k, other, d)
            psend[k, d, 0] = v[:, :128]
            psend[k, d, 1] = v[:, 128:]
            if not started:
                count = 6 + has_after.astype(jnp.int32) + has_before.astype(jnp.int32)
                pl.semaphore_wait(barrier, count)
                started = True
            copies[d] = go(psend.at[k, d], precv.at[k, d], partner)
        return copies

    def for_row(k, from_partner):
        load_wm[k].wait()
        copies = {}
        for d in ORDER:
            v = block(k, mine, d)
            from_partner[d].wait_recv()
            a = v[:, :128] + precv[k, d, 0]
            b = v[:, 128:] + precv[k, d, 1]
            if d == 0:
                acc[k, 0] = a
                acc[k, 1] = b
            else:
                xsend[k, d, 0] = a.astype(BF16)
                xsend[k, d, 1] = b.astype(BF16)
                copies[d] = go(xsend.at[k, d], xrecv.at[k, d], xpeer[d])
        return copies

    zeros[...] = jnp.zeros_like(zeros)
    s0[...] = jnp.zeros_like(s0)
    load_x[UP].wait()
    squares(UP)
    pair_up = for_partner(UP, False)
    mx = go(x.at[UP], xm, mirror)
    load_x[DOWN].wait()
    squares(DOWN)
    sq_pair = go(s0, srp, partner)
    row_up = for_row(UP, pair_up)
    pair_down = for_partner(DOWN, True)
    sq_pair.wait_recv()
    s1[...] = s0[...] + srp[...]
    sq_x = {d: go(s1, srx.at[d], xpeer[d]) for d in (1, 2, 3)}
    row_down = for_row(DOWN, pair_down)

    kk = lax.broadcasted_iota(jnp.int32, (T, QH * T), 0)
    qq = lax.broadcasted_iota(jnp.int32, (T, QH * T), 1)
    for h in range(QH - 1):
        qq = jnp.where(qq >= T, qq - T, qq)
    bias[...] = jnp.where(kk <= qq, 0.0, NEG_BIG)

    for d in (1, 2, 3):
        sq_x[d].wait_recv()
    s2[...] = s1[...] + srx[1] + srx[2] + srx[3]
    sq_z = go(s2, srz, zpeer)

    def for_z(k, row):
        for d in (1, 3, 2):
            row[d].wait_recv()
            acc[k, 0] = acc[k, 0] + xrecv[k, d, 0].astype(F32)
            acc[k, 1] = acc[k, 1] + xrecv[k, d, 1].astype(F32)
        zsend[k] = acc[k, 1 - zi].astype(BF16)
        return go(zsend.at[k], zrecv.at[k], zpeer)

    z_up = for_z(UP, row_up)

    sq_z.wait_recv()
    s3[...] = s2[...] + srz[...]
    sq_m = go(s3, srm, mirror)

    def scale_of(row):
        return column_of(lax.rsqrt(row / D + EPS))

    rcol[UP] = scale_of(s3[0:1, 0:T])
    rcol[DOWN] = scale_of(s3[1:2, 0:T])
    z_down = for_z(DOWN, row_down)

    def final_kv(k, zc):
        zc.wait_recv()
        v = (acc[k, zi] + zrecv[k].astype(F32)) * rcol[k]
        kvf[k] = v
        kv[k, c] = v.astype(BF16)
        return go(kv.at[k, c], kv.at[k, c], partner)

    def attention(k, own):
        load_g[k].wait()
        normed, queries, ups = [], [], []
        for h in range(QH):
            n = x[k, :, h * 128 : h * 128 + 128].astype(F32) * rcol[k]
            queries.append(n.astype(BF16))
            ups.append(g[k, :, h * 128 : h * 128 + 128])
        q = jnp.concatenate(queries, axis=0)
        up = jnp.concatenate(ups, axis=0)
        own.wait_recv()
        key, value = kv[k, 0], kv[k, 1]
        s = dot(key, q, 1, 1) * SCALE + bias[...]
        e = jnp.exp(s - jnp.max(s, axis=0, keepdims=True))
        p = e * (1.0 / jnp.sum(e, axis=0, keepdims=True))
        pl_low = p.astype(BF16)
        dp = dot(value, up, 1, 1)
        ds = p * (dp - jnp.sum(p * dp, axis=0, keepdims=True))
        ds_low = ds.astype(BF16)
        dkv[k, 0] = dot(ds_low, q, 1, 0) * SCALE
        dkv[k, 1] = dot(pl_low, up, 1, 0)
        pair = go(dkv.at[k, 1 - c], dkvr.at[k], partner)
        dqs = dot(ds_low, key, 0, 0) * SCALE
        att = dot(pl_low, value, 0, 0)
        inner = jnp.zeros((T, 128), F32)
        for h in range(QH):
            cols = slice(h * 128, h * 128 + 128)
            rows = slice(h * T, h * T + T)
            xf = x[k, :, cols].astype(F32)
            out[k, :, cols] = (xf + att[rows]).astype(BF16)
            dq[k, h] = dqs[rows]
            inner = inner + dqs[rows] * (xf * rcol[k])
        pair.wait_recv()
        total = dkv[k, c] + dkvr[k]
        low = total.astype(BF16)
        gath[k, c * 8 + head] = low
        i0[k, 0:1, 0:T] = row_of(inner + low.astype(F32) * kvf[k])

    class Gather:
        def __init__(self, k):
            self.k = k
            self.pair = []

        def to(self, b, dev):
            ref = gath.at[self.k, b]
            return go(ref, ref, dev)

        def begin(self):
            b = c * 8 + head
            self.z = self.to(b, zpeer)
            self.x_own = {d: self.to(b, xpeer[d]) for d in (2, 1, 3)}
            self.pair.append(self.to(b, partner))

        def forward_z(self):
            self.z.wait_recv()
            b = c * 8 + xi * 2 + 1 - zi
            self.x_far = {d: self.to(b, xpeer[d]) for d in (2, 1, 3)}
            self.pair.append(self.to(b, partner))

        def forward_x(self, copies, z_):
            for d in (1, 3, 2):
                copies[d].wait_recv()
                b = c * 8 + ((xi + 4 - d) % 4) * 2 + z_
                self.pair.append(self.to(b, partner))

        def finish(self):
            self.forward_x(self.x_own, zi)
            self.forward_x(self.x_far, 1 - zi)

        def arrived(self):
            for copy in self.pair:
                copy.wait_recv()

    def section_send(src, dst, dev, has_to, has_from):
        copy = remote(src, dst, dev)

        @pl.when(has_to)
        def _():
            copy.start()

        return (copy, has_to, has_from)

    crossing = []

    kv_up = final_kv(UP, z_up)
    i0[...] = jnp.zeros_like(i0)
    attention(UP, kv_up)
    up = Gather(UP)
    up.begin()
    inner_z = [go(i0.at[UP], irz.at[UP], zpeer)]
    block_ref = gath.at[UP, c * 8 + head]
    to_mirror = go(block_ref, gath.at[MIRROR, c * 8 + head], mirror)
    crossing.append(section_send(out.at[UP], hu_o, before, has_before, has_after))

    kv_down = final_kv(DOWN, z_down)
    attention(DOWN, kv_down)
    down = Gather(DOWN)
    down.begin()
    inner_z.append(go(i0.at[DOWN], irz.at[DOWN], zpeer))
    crossing.append(section_send(out.at[DOWN], hd_o, after, has_after, has_before))

    def inner_row(k):
        inner_z[k].wait_recv()
        i1[k] = i0[k] + irz[k]
        return {d: go(i1.at[k], irx.at[k, d], xpeer[d]) for d in (1, 2, 3)}

    def inner_pair(k, copies):
        for d in (1, 2, 3):
            copies[d].wait_recv()
        i2[k] = i1[k] + irx[k, 1] + irx[k, 2] + irx[k, 3]
        return go(i2.at[k], irp.at[k], partner)

    up.forward_z()
    ix_up = inner_row(UP)
    to_mirror.wait_recv()
    far = Gather(MIRROR)
    far.begin()
    down.forward_z()
    ix_down = inner_row(DOWN)

    def hidden_rows(v, k, n):
        for h in range(QH):
            cols = slice(h * 128, h * 128 + 128)
            hidt[n, cols, :] = jnp.transpose(v[:, cols].astype(F32) * rcol[k]).astype(BF16)

    hidden_rows(x[DOWN], DOWN, 0)
    sq_m.wait_recv()
    rcol[MIRROR] = scale_of(srm[0:1, 0:T])
    mx.wait_recv()
    hidden_rows(xm[...], MIRROR, 1)
    put_hidt = local(hidt, hidt_o)
    put_hidt.start()

    up.finish()
    ip_up = inner_pair(UP, ix_up)
    far.forward_z()

    def grad_input(k, ip):
        ip.wait_recv()
        mean = column_of((i2[k, 0:1, 0:T] + irp[k, 0:1, 0:T]) * (1.0 / D))
        r = rcol[k]
        for n in range(2):
            rows = slice(n * 256, n * 256 + 256)
            total = jnp.concatenate([dq[k, 2 * n], dq[k, 2 * n + 1]], axis=1)
            for b in range(0, 16, 2):
                pair = jnp.concatenate([gath[k, b], gath[k, b + 1]], axis=1)
                total = total + dot(pair, w[k, rows, b * 128 : b * 128 + 256], 1, 1)
            for m in range(2):
                cols = slice(n * 256 + m * 128, n * 256 + m * 128 + 128)
                gh = total[:, m * 128 : m * 128 + 128]
                normed = x[k, :, cols].astype(F32) * r
                gin[k, :, cols] = (g[k, :, cols].astype(F32) + r * (gh - normed * mean)).astype(BF16)

    up.arrived()
    grad_input(UP, ip_up)
    crossing.append(section_send(gin.at[UP], ru_o, after, has_after, has_before))

    down.finish()
    ip_down = inner_pair(DOWN, ix_down)
    down.arrived()
    grad_input(DOWN, ip_down)
    crossing.append(section_send(gin.at[DOWN], rd_o, before, has_before, has_after))
    put_down = local(gath.at[DOWN], gath_o.at[0])
    put_down.start()

    far.finish()
    far.arrived()
    put_far = local(gath.at[MIRROR], gath_o.at[1])
    put_far.start()

    blank = [local(zeros, ref) for ref in (hu_o, ru_o, hd_o, rd_o)]
    ends = (sec == sections - 1, sec == 0, sec == 0, sec == sections - 1)
    for copy, here in zip(blank, ends):

        @pl.when(here)
        def _(copy=copy):
            copy.start()

    put_hidt.wait()
    put_down.wait()
    put_far.wait()
    for copy, here in zip(blank, ends):

        @pl.when(here)
        def _(copy=copy):
            copy.wait()

    for copy, has_to, has_from in crossing:

        @pl.when(has_to)
        def _(copy=copy):
            copy.wait_send()

        @pl.when(has_from)
        def _(copy=copy):
            copy.wait_recv()

    for copy in sends:
        copy.wait_send()


def exchange(sections, xd, xu, gd, gu, wd, wu):
    act = jax.ShapeDtypeStruct((T, W), BF16)
    hbm = pl.BlockSpec(memory_space=pltpu.HBM)
    free = pl.BlockSpec(memory_space=pl.ANY)
    V = pltpu.VMEM
    small = (8, LANES)
    scratch = [
        V((2, T, W), BF16), V((2, T, W), BF16), V((2, W, 2 * HALF), BF16), V((T, W), BF16),
        V((T, QH * T), F32), V((T, W), BF16), V((2, W, T), BF16),
        V((2, 4, 2, T, 128), F32), V((2, 4, 2, T, 128), F32),
        V((2, 4, 2, T, 128), BF16), V((2, 4, 2, T, 128), BF16),
        V((2, 2, T, 128), F32), V((2, T, 128), BF16), V((2, T, 128), BF16),
        V((2, T, 128), F32), V((2, 2, T, 128), BF16), V((3, T, 128), F32),
        V((2, QH, T, 128), F32), V((2, 2, T, 128), F32), V((2, T, 128), F32),
        V((3, 16, T, 128), BF16), V((2, T, W), BF16), V((2, T, W), BF16),
        V(small, F32), V(small, F32), V(small, F32), V(small, F32),
        V(small, F32), V((4,) + small, F32), V(small, F32), V(small, F32),
        V((2,) + small, F32), V((2,) + small, F32), V((2,) + small, F32),
        V((2,) + small, F32), V((2, 4) + small, F32), V((2,) + small, F32),
        pltpu.SemaphoreType.DMA((16,)), pltpu.SemaphoreType.DMA((104,)), pltpu.SemaphoreType.DMA((104,)),
    ]

    def kernel(*refs):
        exchange_kernel(sections, *refs)

    return pl.pallas_call(
        kernel,
        out_shape=(act, act, act, act, jax.ShapeDtypeStruct((2, W, T), BF16),
                   jax.ShapeDtypeStruct((2, 16, T, 128), BF16)),
        in_specs=[hbm] * 6,
        out_specs=(free,) * 6,
        scratch_shapes=scratch,
        name="exchange",
        compiler_params=pltpu.CompilerParams(
            collective_id=0, has_side_effects=True, vmem_limit_bytes=58 << 20),
    )(xd, xu, gd, gu, wd, wu)


def weights_kernel(hidt, gath, a, b, c, d, dw, ao, bo, co, do):
    for n in range(2):
        total = jnp.zeros((W, 256), F32)
        for m in range(2):
            pair = jnp.concatenate([gath[m, 2 * n], gath[m, 2 * n + 1]], axis=1)
            total = total + dot(hidt[m], pair, 1, 0)
        dw[:, n * 256 : n * 256 + 256] = total
    for src, dst in ((a, ao), (b, bo), (c, co), (d, do)):
        dst[...] = src[...]


def weight_sums(hidt, gath, arrays):
    act = jax.ShapeDtypeStruct((T, W), BF16)
    piece = pl.BlockSpec((T, 128), lambda i: (0, i))
    return pl.pallas_call(
        weights_kernel,
        grid=(4,),
        out_shape=(jax.ShapeDtypeStruct((W, 2 * HALF), F32),) + (act,) * 4,
        in_specs=[pl.BlockSpec((2, W, T), lambda i: (0, 0, 0)),
                  pl.BlockSpec((2, 4, T, 128), lambda i: (0, i, 0, 0))] + [piece] * 4,
        out_specs=(pl.BlockSpec((W, 512), lambda i: (0, i)),) + (piece,) * 4,
        name="weight_sums",
        compiler_params=pltpu.CompilerParams(
            dimension_semantics=("arbitrary",), vmem_limit_bytes=24 << 20),
    )(hidt, gath, *arrays)


def solution(mesh):
    sections = mesh.shape["section"]

    def on_device(xd, xu, gd, gu, wd, wu):
        *arrays, hidt, gath = exchange(sections, xd[0], xu[0], gd[0], gu[0], wd[0], wu[0])
        dw, hd, hu, rd, ru = weight_sums(hidt, gath, arrays)
        return hd[None], hu[None], rd[None], ru[None], dw[None]

    act, wts = P("section", None, "tensor"), P("section", "tensor", None)
    return jax.shard_map(
        on_device, mesh=mesh, in_specs=(act,) * 4 + (wts,) * 2,
        out_specs=(act,) * 4 + (wts,), check_vma=False)
```

```python
import jax
import jax.numpy as jnp
from jax import lax
from jax.experimental import pallas as pl
from jax.experimental.pallas import tpu as pltpu
from jax.sharding import PartitionSpec as P

MESH = pl.DeviceIdType.MESH
F32 = jnp.float32
BF16 = jnp.bfloat16

D = 8192
HEAD_DIM = 128
EPS = 1e-05
NEG_BIG = -1e30
SCALE = HEAD_DIM ** (-0.5)

T = 224
W = 512
HALF = 1024
QH = W // HEAD_DIM
LANES = 256

UP, DOWN, MIRROR = 0, 1, 2


def dot(a, b, ca, cb):
    return lax.dot_general(a, b, (((ca,), (cb,)), ((), ())), preferred_element_type=F32)


def row_of(total):
    return jnp.sum(jnp.transpose(total), axis=0, keepdims=True)


def column_of(row):
    return jnp.transpose(jnp.broadcast_to(row, (128, T)))


def exchange_kernel(sections, *refs):
    (xd_h, xu_h, gd_h, gu_h, wd_h, wu_h) = refs[:6]
    (hd_o, hu_o, rd_o, ru_o, hidt, gath_o) = refs[6:12]
    (x, g, w, xm, bias) = refs[12:17]
    (psend, precv, xsend, xrecv, acc, zsend, zrecv, kvf, kv, rcol) = refs[17:27]
    (dq, dkv, dkvr, gath_up, out, gin) = refs[27:33]
    gh = refs[50]
    (s0, s1, s2, s3, srp, srx, srz, srm) = refs[33:41]
    (i0, i1, i2, irz, irx, irp) = refs[41:47]
    (lsem, ssem, rsem) = refs[47:50]

    gath = (gath_up, gath_o.at[0], gath_o.at[1])

    sec = lax.axis_index("section")
    t = lax.axis_index("tensor")
    xi, zi, c = t // 4, (t // 2) % 2, t % 2
    mine, other = c * HALF, (1 - c) * HALF
    head = xi * 2 + zi

    def at(x_, z_, c_):
        return (sec, x_ * 4 + z_ * 2 + c_)

    partner = at(xi, zi, 1 - c)
    zpeer = at(xi, 1 - zi, c)
    xpeer = {d: at((xi + d) % 4, zi, c) for d in (1, 2, 3)}
    mirror = (sections - 1 - sec, t)
    mirror_z = (sections - 1 - sec, xi * 4 + (1 - zi) * 2 + c)
    after = (lax.rem(sec + 1, sections), t)
    before = (lax.rem(sec + sections - 1, sections), t)
    has_after = sec < sections - 1
    has_before = sec > 0

    used = [0, 0]

    def remote(src, dst, dev):
        n = used[0]
        used[0] += 1
        return pltpu.make_async_remote_copy(
            src_ref=src, dst_ref=dst, send_sem=ssem.at[n], recv_sem=rsem.at[n],
            device_id=dev, device_id_type=MESH)

    def local(src, dst):
        n = used[1]
        used[1] += 1
        return pltpu.make_async_copy(src, dst, lsem.at[n])

    sends = []

    def go(src, dst, dev):
        copy = remote(src, dst, dev)
        copy.start()
        sends.append(copy)
        return copy

    barrier = pltpu.get_barrier_semaphore()
    for dev in (partner, zpeer, xpeer[1], xpeer[2], xpeer[3], mirror, mirror_z):
        pl.semaphore_signal(barrier, inc=1, device_id=dev, device_id_type=MESH)

    @pl.when(has_after)
    def _():
        pl.semaphore_signal(barrier, inc=1, device_id=after, device_id_type=MESH)

    @pl.when(has_before)
    def _():
        pl.semaphore_signal(barrier, inc=1, device_id=before, device_id_type=MESH)

    load_x = [local(xu_h, x.at[UP]), local(xd_h, x.at[DOWN])]
    load_g = [local(gu_h, g.at[UP]), local(gd_h, g.at[DOWN])]
    mcols, ocols = pl.ds(pl.multiple_of(mine, HALF), HALF), pl.ds(pl.multiple_of(other, HALF), HALF)
    wh = (wu_h, wd_h)
    load_wo = [local(wh[k].at[:, ocols], w.at[k, :, ocols]) for k in (UP, DOWN)]
    load_wm = [local(wh[k].at[:, mcols], w.at[k, :, mcols]) for k in (UP, DOWN)]
    load_x[UP].start()
    load_x[DOWN].start()
    load_wo[UP].start()
    load_wm[UP].start()
    load_wo[DOWN].start()
    load_wm[DOWN].start()
    load_g[UP].start()
    load_g[DOWN].start()

    FAR, NEAR = 0, 1
    PAIRS = ((2, 1), (3, 0))

    def block(k, base, side, ds):
        z_ = 1 - zi if side == FAR else zi
        cols = [pl.multiple_of(base + ((xi + d) % 4) * 256 + z_ * 128, 128) for d in ds]
        return dot(x[k], jnp.concatenate([w[k, :, pl.ds(n, 128)] for n in cols], axis=1), 1, 0)

    def squares(k):
        v = x[k].astype(F32)
        v = v * v
        total = v[:, 0:128] + v[:, 128:256] + v[:, 256:384] + v[:, 384:512]
        s0[k : k + 1, 0:T] = row_of(total)

    def for_partner(k, side, first=lambda: None):
        copies = []
        for n, ds in enumerate(PAIRS):
            v = block(k, other, side, ds)
            m = side * 2 + n
            psend[k, m, 0] = v[:, :128]
            psend[k, m, 1] = v[:, 128:]
            if n == 0:
                first()
            copies.append(go(psend.at[k, m], precv.at[k, m], partner))
        return copies

    def for_row(k, side, from_partner, first=lambda: None):
        first()
        for n, ds in enumerate(PAIRS):
            v = block(k, mine, side, ds)
            from_partner[n].wait_recv()
            for i, d in enumerate(ds):
                part = v[:, i * 128 : i * 128 + 128] + precv[k, side * 2 + n, i]
                if d == 0:
                    acc[k, side] = part
                else:
                    xsend[k, side, d] = part.astype(BF16)
        return (2, 1, 3)

    def send_row(k, side, ds):
        return {d: go(xsend.at[k, side, d], xrecv.at[k, side, d], xpeer[d]) for d in ds}

    s0[...] = jnp.zeros_like(s0)
    early = {}

    def after_entry():
        count = 7 + has_after.astype(jnp.int32) + has_before.astype(jnp.int32)
        pl.semaphore_wait(barrier, count)
        early["mx"] = go(x.at[UP], xm, mirror)
        early["sq"] = go(s0, srp, partner)

    def spread_squares():
        early["sq"].wait_recv()
        s1[...] = s0[...] + srp[...]
        early["sq_x"] = {d: go(s1, srx.at[d], xpeer[d]) for d in (1, 2, 3)}

    load_x[UP].wait()
    squares(UP)
    load_x[DOWN].wait()
    squares(DOWN)
    pair, held, row = {}, {}, {}
    load_wo[UP].wait()
    pair[UP, FAR] = for_partner(UP, FAR, after_entry)
    load_wm[UP].wait()
    row[UP, FAR] = send_row(UP, FAR, for_row(UP, FAR, pair[UP, FAR], spread_squares))
    load_wo[DOWN].wait()
    pair[DOWN, FAR] = for_partner(DOWN, FAR)
    pair[UP, NEAR] = for_partner(UP, NEAR)
    load_wm[DOWN].wait()
    held[DOWN, FAR] = for_row(DOWN, FAR, pair[DOWN, FAR])
    row[DOWN, FAR] = send_row(DOWN, FAR, held[DOWN, FAR])
    pair[DOWN, NEAR] = for_partner(DOWN, NEAR)
    held[UP, NEAR] = for_row(UP, NEAR, pair[UP, NEAR])
    sq_x = early["sq_x"]
    for d in (1, 2, 3):
        sq_x[d].wait_recv()
    s2[...] = s1[...] + srx[1] + srx[2] + srx[3]
    sq_z = go(s2, srz, zpeer)
    held[DOWN, NEAR] = for_row(DOWN, NEAR, pair[DOWN, NEAR])

    kk = lax.broadcasted_iota(jnp.int32, (T, QH * T), 0)
    qq = lax.broadcasted_iota(jnp.int32, (T, QH * T), 1)
    for h in range(QH - 1):
        qq = jnp.where(qq >= T, qq - T, qq)
    bias[...] = jnp.where(kk <= qq, 0.0, NEG_BIG)

    def gathered(k, side):
        for d in (1, 3, 2):
            row[k, side][d].wait_recv()
        parts = [xrecv[k, side, d].astype(F32) for d in (1, 3, 2)]
        return acc[k, side] + parts[0] + parts[1] + parts[2]

    def for_z(k):
        zsend[k] = gathered(k, FAR).astype(BF16)
        return go(zsend.at[k], zrecv.at[k], zpeer)

    z_up = for_z(UP)
    row[UP, NEAR] = send_row(UP, NEAR, held[UP, NEAR])
    z_down = for_z(DOWN)
    row[DOWN, NEAR] = send_row(DOWN, NEAR, held[DOWN, NEAR])
    sq_z.wait_recv()
    s3[...] = s2[...] + srz[...]
    sq_m = go(s3, srm, mirror)

    def scale_of(row):
        return column_of(lax.rsqrt(row / D + EPS))

    rcol[UP] = scale_of(s3[0:1, 0:T])
    rcol[DOWN] = scale_of(s3[1:2, 0:T])

    def final_kv(k, zc):
        near = gathered(k, NEAR)
        zc.wait_recv()
        v = (near + zrecv[k].astype(F32)) * rcol[k]
        kvf[k] = v
        kv[k, c] = v.astype(BF16)
        return go(kv.at[k, c], kv.at[k, c], partner)

    def attention(k, own):
        load_g[k].wait()
        normed, queries, ups = [], [], []
        for h in range(QH):
            n = x[k, :, h * 128 : h * 128 + 128].astype(F32) * rcol[k]
            queries.append(n.astype(BF16))
            ups.append(g[k, :, h * 128 : h * 128 + 128])
        q = jnp.concatenate(queries, axis=0)
        up = jnp.concatenate(ups, axis=0)
        own.wait_recv()
        key, value = kv[k, 0], kv[k, 1]
        s = dot(key, q, 1, 1) * SCALE + bias[...]
        e = jnp.exp(s - jnp.max(s, axis=0, keepdims=True))
        p = e * (1.0 / jnp.sum(e, axis=0, keepdims=True))
        pl_low = p.astype(BF16)
        dp = dot(value, up, 1, 1)
        ds = p * (dp - jnp.sum(p * dp, axis=0, keepdims=True))
        ds_low = ds.astype(BF16)
        dkv[k, 0] = dot(ds_low, q, 1, 0) * SCALE
        dkv[k, 1] = dot(pl_low, up, 1, 0)
        pair = go(dkv.at[k, 1 - c], dkvr.at[k], partner)
        dqs = dot(ds_low, key, 0, 0) * SCALE
        att = dot(pl_low, value, 0, 0)
        inner = jnp.zeros((T, 128), F32)
        for h in range(QH):
            cols = slice(h * 128, h * 128 + 128)
            rows = slice(h * T, h * T + T)
            xf = x[k, :, cols].astype(F32)
            out[k, :, cols] = (xf + att[rows]).astype(BF16)
            dq[k, h] = dqs[rows]
            inner = inner + dqs[rows] * (xf * rcol[k])
        pair.wait_recv()
        total = dkv[k, c] + dkvr[k]
        low = total.astype(BF16)
        gath[k][c * 8 + head] = low
        i0[k, 0:1, 0:T] = row_of(inner + low.astype(F32) * kvf[k])

    class Gather:
        def __init__(self, k):
            self.k = k
            self.pair = {0: [], 1: []}

        def to(self, b, dev):
            ref = gath[self.k].at[b]
            return go(ref, ref, dev)

        def begin(self):
            b = c * 8 + head
            if self.k != MIRROR:
                self.z = self.to(b, zpeer)
            self.x_own = {d: self.to(b, xpeer[d]) for d in (2, 1, 3)}
            self.pair[0].append(self.to(b, partner))

        def forward_z(self):
            if self.k != MIRROR:
                self.z.wait_recv()
            b = c * 8 + xi * 2 + 1 - zi
            self.x_far = {d: self.to(b, xpeer[d]) for d in (2, 1, 3)}
            self.pair[1].append(self.to(b, partner))

        def forward_x(self, n):
            copies, z_ = (self.x_far, 1 - zi) if n else (self.x_own, zi)
            for d in (1, 3, 2):
                copies[d].wait_recv()
                b = c * 8 + ((xi + 4 - d) % 4) * 2 + z_
                self.pair[n].append(self.to(b, partner))

        def arrived(self, n):
            for copy in self.pair[n]:
                copy.wait_recv()

    def section_send(src, dst, dev, has_to, has_from):
        copy = remote(src, dst, dev)

        @pl.when(has_to)
        def _():
            copy.start()

        return (copy, has_to, has_from)

    crossing = []

    kv_up = final_kv(UP, z_up)
    i0[...] = jnp.zeros_like(i0)
    attention(UP, kv_up)
    up = Gather(UP)
    up.begin()
    inner_z = [go(i0.at[UP], irz.at[UP], zpeer)]

    kv_down = final_kv(DOWN, z_down)
    attention(DOWN, kv_down)
    down = Gather(DOWN)
    down.begin()
    inner_z.append(go(i0.at[DOWN], irz.at[DOWN], zpeer))

    def inner_row(k):
        inner_z[k].wait_recv()
        i1[k] = i0[k] + irz[k]
        return {d: go(i1.at[k], irx.at[k, d], xpeer[d]) for d in (1, 2, 3)}

    def inner_pair(k, copies):
        for d in (1, 2, 3):
            copies[d].wait_recv()
        i2[k] = i1[k] + irx[k, 1] + irx[k, 2] + irx[k, 3]
        return go(i2.at[k], irp.at[k], partner)

    def part_of(k, n, blocks, total):
        rows = slice(n * 256, n * 256 + 256)
        pair = jnp.concatenate([gath[k][b] for b in blocks], axis=1)
        cols = [pl.multiple_of(b * 128, 128) for b in blocks]
        rhs = jnp.concatenate([w[k, rows, pl.ds(b, 128)] for b in cols], axis=1)
        return total + dot(pair, rhs, 1, 1)

    def grad_near(k):
        for n in range(2):
            total = jnp.concatenate([dq[k, 2 * n], dq[k, 2 * n + 1]], axis=1)
            for i in range(4):
                total = part_of(k, n, [i * 2 + zi, 8 + i * 2 + zi], total)
            gh[k, n] = total

    def grad_input(k, ip, target, dev, has_to, has_from):
        ip.wait_recv()
        mean = column_of((i2[k, 0:1, 0:T] + irp[k, 0:1, 0:T]) * (1.0 / D))
        r = rcol[k]
        for n in range(2):
            total = gh[k, n]
            for i in range(4):
                total = part_of(k, n, [i * 2 + 1 - zi, 9 + i * 2 - zi], total)
            for m in range(2):
                cols = slice(n * 256 + m * 128, n * 256 + m * 128 + 128)
                normed = x[k, :, cols].astype(F32) * r
                value = total[:, m * 128 : m * 128 + 128] - normed * mean
                gin[k, :, cols] = (g[k, :, cols].astype(F32) + r * value).astype(BF16)
            cols = slice(n * 256, n * 256 + 256)
            crossing.append(section_send(gin.at[k, :, cols], target.at[:, cols], dev, has_to, has_from))

    def hidden_rows(v, k, n):
        for h in range(QH):
            cols = slice(h * 128, h * 128 + 128)
            hidt[n, cols, :] = jnp.transpose(v[:, cols].astype(F32) * rcol[k]).astype(BF16)

    hidden_rows(x[DOWN], DOWN, 0)
    sq_m.wait_recv()
    rcol[MIRROR] = scale_of(srm[0:1, 0:T])
    early["mx"].wait_recv()
    hidden_rows(xm[...], MIRROR, 1)
    up.forward_z()
    ix_up = inner_row(UP)
    ref = gath[UP].at[c * 8 + head]
    to_mirror = [go(ref, gath[MIRROR].at[c * 8 + head], dev) for dev in (mirror, mirror_z)]
    up.forward_x(0)
    up.arrived(0)
    grad_near(UP)
    down.forward_x(0)
    down.forward_z()
    ix_down = inner_row(DOWN)
    crossing.append(section_send(out.at[UP], hu_o, before, has_before, has_after))
    crossing.append(section_send(out.at[DOWN], hd_o, after, has_after, has_before))
    down.arrived(0)
    grad_near(DOWN)
    up.forward_x(1)
    ip_up = inner_pair(UP, ix_up)
    up.arrived(1)
    grad_input(UP, ip_up, ru_o, after, has_after, has_before)
    far = Gather(MIRROR)
    to_mirror[0].wait_recv()
    far.begin()
    to_mirror[1].wait_recv()
    far.forward_z()
    down.forward_x(1)
    ip_down = inner_pair(DOWN, ix_down)
    down.arrived(1)
    grad_input(DOWN, ip_down, rd_o, before, has_before, has_after)
    far.forward_x(0)
    far.forward_x(1)
    far.arrived(0)
    far.arrived(1)

    for ref, here in ((hu_o, sec == sections - 1), (ru_o, sec == 0), (hd_o, sec == 0), (rd_o, sec == sections - 1)):

        @pl.when(here)
        def _(ref=ref):
            ref[...] = jnp.zeros_like(ref)

    for copy, has_to, has_from in crossing:

        @pl.when(has_to)
        def _(copy=copy):
            copy.wait_send()

        @pl.when(has_from)
        def _(copy=copy):
            copy.wait_recv()

    for copy in sends:
        copy.wait_send()


def exchange(sections, xd, xu, gd, gu, wd, wu):
    act = pltpu.VMEM((T, W), BF16)
    hbm = pl.BlockSpec(memory_space=pltpu.HBM)
    vmem = pl.BlockSpec(memory_space=pltpu.VMEM)
    V = pltpu.VMEM
    small = (8, LANES)
    scratch = [
        V((2, T, W), BF16), V((2, T, W), BF16), V((2, W, 2 * HALF), BF16), V((T, W), BF16),
        V((T, QH * T), F32),
        V((2, 4, 2, T, 128), F32), V((2, 4, 2, T, 128), F32),
        V((2, 2, 4, T, 128), BF16), V((2, 2, 4, T, 128), BF16),
        V((2, 2, T, 128), F32), V((2, T, 128), BF16), V((2, T, 128), BF16),
        V((2, T, 128), F32), V((2, 2, T, 128), BF16), V((3, T, 128), F32),
        V((2, QH, T, 128), F32), V((2, 2, T, 128), F32), V((2, T, 128), F32),
        V((16, T, 128), BF16), V((2, T, W), BF16), V((2, T, W), BF16),
        V(small, F32), V(small, F32), V(small, F32), V(small, F32),
        V(small, F32), V((4,) + small, F32), V(small, F32), V(small, F32),
        V((2,) + small, F32), V((2,) + small, F32), V((2,) + small, F32),
        V((2,) + small, F32), V((2, 4) + small, F32), V((2,) + small, F32),
        pltpu.SemaphoreType.DMA((8,)), pltpu.SemaphoreType.DMA((104,)), pltpu.SemaphoreType.DMA((104,)),
        V((2, 2, T, 256), F32),
    ]

    def kernel(*refs):
        exchange_kernel(sections, *refs)

    return pl.pallas_call(
        kernel,
        out_shape=(act, act, act, act, pltpu.VMEM((2, W, T), BF16),
                   pltpu.VMEM((2, 16, T, 128), BF16)),
        in_specs=[hbm] * 6,
        out_specs=(vmem,) * 6,
        scratch_shapes=scratch,
        name="exchange",
        compiler_params=pltpu.CompilerParams(
            collective_id=0, has_side_effects=True, vmem_limit_bytes=58 << 20),
    )(xd, xu, gd, gu, wd, wu)


def weights_kernel(hidt, gath, a, b, c, d, dw, ao, bo, co, do):
    for n in range(2):
        total = jnp.zeros((W, 256), F32)
        for m in range(2):
            pair = jnp.concatenate([gath[m, 2 * n], gath[m, 2 * n + 1]], axis=1)
            total = total + dot(hidt[m], pair, 1, 0)
        dw[:, n * 256 : n * 256 + 256] = total
    for src, dst in ((a, ao), (b, bo), (c, co), (d, do)):
        dst[...] = src[...]


def weight_sums(hidt, gath, arrays):
    act = jax.ShapeDtypeStruct((T, W), BF16)
    piece = pl.BlockSpec((T, 128), lambda i: (0, i))
    return pl.pallas_call(
        weights_kernel,
        grid=(4,),
        out_shape=(jax.ShapeDtypeStruct((W, 2 * HALF), F32),) + (act,) * 4,
        in_specs=[pl.BlockSpec((2, W, T), lambda i: (0, 0, 0)),
                  pl.BlockSpec((2, 4, T, 128), lambda i: (0, i, 0, 0))] + [piece] * 4,
        out_specs=(pl.BlockSpec((W, 512), lambda i: (0, i)),) + (piece,) * 4,
        name="weight_sums",
        compiler_params=pltpu.CompilerParams(
            dimension_semantics=("arbitrary",), vmem_limit_bytes=24 << 20),
    )(hidt, gath, *arrays)


def solution(mesh):
    sections = mesh.shape["section"]

    def on_device(xd, xu, gd, gu, wd, wu):
        *arrays, hidt, gath = exchange(sections, xd[0], xu[0], gd[0], gu[0], wd[0], wu[0])
        dw, hd, hu, rd, ru = weight_sums(hidt, gath, arrays)
        return hd[None], hu[None], rd[None], ru[None], dw[None]

    act, wts = P("section", None, "tensor"), P("section", "tensor", None)
    return jax.shard_map(
        on_device, mesh=mesh, in_specs=(act,) * 4 + (wts,) * 2,
        out_specs=(act,) * 4 + (wts,), check_vma=False)
```

```python
import jax
import jax.numpy as jnp
from jax import lax
from jax.experimental import pallas as pl
from jax.experimental.pallas import tpu as pltpu
from jax.sharding import PartitionSpec as P

MESH = pl.DeviceIdType.MESH
F32 = jnp.float32
BF16 = jnp.bfloat16

D = 8192
HEAD_DIM = 128
EPS = 1e-05
NEG_BIG = -1e30
SCALE = HEAD_DIM ** (-0.5)

T = 224
W = 512
HALF = 1024
QH = W // HEAD_DIM
LANES = 256

UP, DOWN, MIRROR = 0, 1, 2
LOADS, SENDS, COPIES = 8, 58, 95


def dot(a, b, ca, cb):
    return lax.dot_general(a, b, (((ca,), (cb,)), ((), ())), preferred_element_type=F32)


def row_of(total):
    return jnp.sum(jnp.transpose(total), axis=0, keepdims=True)


def column_of(row):
    return jnp.transpose(jnp.broadcast_to(row, (128, T)))


def exchange_kernel(sections, *refs):
    (xd_h, xu_h, gd_h, gu_h, wd_h, wu_h) = refs[:6]
    (hd_o, hu_o, rd_o, ru_o, hidt, gath_o) = refs[6:12]
    (x, g, w, xm, bias) = refs[12:17]
    (psend, precv, xsend, xrecv, acc, zsend, zrecv, kvf, kv, rcol) = refs[17:27]
    (dq, dkv, dkvr, gath_up, out, gin) = refs[27:33]
    gh = refs[50]
    (s0, s1, s2, s3, srp, srx, srz, srm) = refs[33:41]
    (i0, i1, i2, irz, irx, irp) = refs[41:47]
    (lsem, ssem, rsem) = refs[47:50]

    gath = (gath_up, gath_o.at[0], gath_o.at[1])

    sec = lax.axis_index("section")
    t = lax.axis_index("tensor")
    xi, zi, c = t // 4, (t // 2) % 2, t % 2
    mine, other = c * HALF, (1 - c) * HALF
    head = xi * 2 + zi

    def at(x_, z_, c_):
        return (sec, x_ * 4 + z_ * 2 + c_)

    partner = at(xi, zi, 1 - c)
    zpeer = at(xi, 1 - zi, c)
    xpeer = {d: at((xi + d) % 4, zi, c) for d in (1, 2, 3)}
    mirror = (sections - 1 - sec, t)
    mirror_z = (sections - 1 - sec, xi * 4 + (1 - zi) * 2 + c)
    after = (lax.rem(sec + 1, sections), t)
    before = (lax.rem(sec + sections - 1, sections), t)
    has_after = sec < sections - 1
    has_before = sec > 0

    used = [0, 0, 0]
    idle = []

    def remote(src, dst, dev, m=None):
        n = used[0]
        used[0] += 1
        if m is None:
            m = used[2]
            used[2] += 1
        return pltpu.make_async_remote_copy(
            src_ref=src, dst_ref=dst, send_sem=ssem.at[m], recv_sem=rsem.at[n],
            device_id=dev, device_id_type=MESH)

    def local(src, dst):
        n = used[1]
        used[1] += 1
        return pltpu.make_async_copy(src, dst, lsem.at[n])

    sends = []

    def go(src, dst, dev):
        if idle:
            m = idle.pop()
        else:
            m = used[2]
            used[2] += 1
        copy = remote(src, dst, dev, m)
        copy.start()
        sends.append((copy, m))
        return copy

    def drain(count):
        for copy, m in sends[:count]:
            copy.wait_send()
            idle.append(m)
        del sends[:count]

    barrier = pltpu.get_barrier_semaphore()
    for dev in (partner, zpeer, xpeer[1], xpeer[2], xpeer[3], mirror, mirror_z):
        pl.semaphore_signal(barrier, inc=1, device_id=dev, device_id_type=MESH)

    @pl.when(has_after)
    def _():
        pl.semaphore_signal(barrier, inc=1, device_id=after, device_id_type=MESH)

    @pl.when(has_before)
    def _():
        pl.semaphore_signal(barrier, inc=1, device_id=before, device_id_type=MESH)

    load_x = [local(xu_h, x.at[UP]), local(xd_h, x.at[DOWN])]
    load_g = [local(gu_h, g.at[UP]), local(gd_h, g.at[DOWN])]
    mcols, ocols = pl.ds(pl.multiple_of(mine, HALF), HALF), pl.ds(pl.multiple_of(other, HALF), HALF)
    wh = (wu_h, wd_h)
    load_wo = [local(wh[k].at[:, ocols], w.at[k, :, ocols]) for k in (UP, DOWN)]
    load_wm = [local(wh[k].at[:, mcols], w.at[k, :, mcols]) for k in (UP, DOWN)]
    load_x[UP].start()
    load_x[DOWN].start()
    load_wo[UP].start()
    load_wm[UP].start()
    load_wo[DOWN].start()
    load_wm[DOWN].start()
    load_g[UP].start()
    load_g[DOWN].start()

    FAR, NEAR = 0, 1
    PAIRS = ((2, 1), (3, 0))

    def block(k, base, side, ds):
        z_ = 1 - zi if side == FAR else zi
        cols = [pl.multiple_of(base + ((xi + d) % 4) * 256 + z_ * 128, 128) for d in ds]
        return dot(x[k], jnp.concatenate([w[k, :, pl.ds(n, 128)] for n in cols], axis=1), 1, 0)

    def squares(k):
        v = x[k].astype(F32)
        v = v * v
        total = v[:, 0:128] + v[:, 128:256] + v[:, 256:384] + v[:, 384:512]
        s0[k : k + 1, 0:T] = row_of(total)

    def for_partner(k, side, first=lambda: None):
        copies = []
        for n, ds in enumerate(PAIRS):
            v = block(k, other, side, ds)
            m = side * 2 + n
            psend[k, m, 0] = v[:, :128]
            psend[k, m, 1] = v[:, 128:]
            if n == 0:
                first()
            copies.append(go(psend.at[k, m], precv.at[k, m], partner))
        return copies

    def for_row(k, side, from_partner, first=lambda: None):
        first()
        for n, ds in enumerate(PAIRS):
            v = block(k, mine, side, ds)
            from_partner[n].wait_recv()
            for i, d in enumerate(ds):
                part = v[:, i * 128 : i * 128 + 128] + precv[k, side * 2 + n, i]
                if d == 0:
                    acc[k, side] = part
                else:
                    xsend[k, side, d] = part.astype(BF16)
        return (2, 1, 3)

    def send_row(k, side, ds):
        return {d: go(xsend.at[k, side, d], xrecv.at[k, side, d], xpeer[d]) for d in ds}

    s0[...] = jnp.zeros_like(s0)
    early = {}

    def after_entry():
        count = 7 + has_after.astype(jnp.int32) + has_before.astype(jnp.int32)
        pl.semaphore_wait(barrier, count)
        early["mx"] = go(x.at[UP], xm, mirror)
        early["sq"] = go(s0, srp, partner)

    def spread_squares():
        early["sq"].wait_recv()
        s1[...] = s0[...] + srp[...]
        early["sq_x"] = {d: go(s1, srx.at[d], xpeer[d]) for d in (1, 2, 3)}

    load_x[UP].wait()
    squares(UP)
    load_x[DOWN].wait()
    squares(DOWN)
    pair, held, row = {}, {}, {}
    load_wo[UP].wait()
    pair[UP, FAR] = for_partner(UP, FAR, after_entry)
    load_wm[UP].wait()
    row[UP, FAR] = send_row(UP, FAR, for_row(UP, FAR, pair[UP, FAR], spread_squares))
    load_wo[DOWN].wait()
    pair[DOWN, FAR] = for_partner(DOWN, FAR)
    pair[UP, NEAR] = for_partner(UP, NEAR)
    load_wm[DOWN].wait()
    held[DOWN, FAR] = for_row(DOWN, FAR, pair[DOWN, FAR])
    row[DOWN, FAR] = send_row(DOWN, FAR, held[DOWN, FAR])
    pair[DOWN, NEAR] = for_partner(DOWN, NEAR)
    held[UP, NEAR] = for_row(UP, NEAR, pair[UP, NEAR])
    sq_x = early["sq_x"]
    for d in (1, 2, 3):
        sq_x[d].wait_recv()
    s2[...] = s1[...] + srx[1] + srx[2] + srx[3]
    sq_z = go(s2, srz, zpeer)
    held[DOWN, NEAR] = for_row(DOWN, NEAR, pair[DOWN, NEAR])

    kk = lax.broadcasted_iota(jnp.int32, (T, QH * T), 0)
    qq = lax.broadcasted_iota(jnp.int32, (T, QH * T), 1)
    for h in range(QH - 1):
        qq = jnp.where(qq >= T, qq - T, qq)
    bias[...] = jnp.where(kk <= qq, 0.0, NEG_BIG)

    def gathered(k, side):
        for d in (1, 3, 2):
            row[k, side][d].wait_recv()
        parts = [xrecv[k, side, d].astype(F32) for d in (1, 3, 2)]
        return acc[k, side] + parts[0] + parts[1] + parts[2]

    def for_z(k):
        zsend[k] = gathered(k, FAR).astype(BF16)
        return go(zsend.at[k], zrecv.at[k], zpeer)

    z_up = for_z(UP)
    row[UP, NEAR] = send_row(UP, NEAR, held[UP, NEAR])
    z_down = for_z(DOWN)
    row[DOWN, NEAR] = send_row(DOWN, NEAR, held[DOWN, NEAR])
    sq_z.wait_recv()
    s3[...] = s2[...] + srz[...]
    sq_m = go(s3, srm, mirror)

    def scale_of(row):
        return column_of(lax.rsqrt(row / D + EPS))

    rcol[UP] = scale_of(s3[0:1, 0:T])
    rcol[DOWN] = scale_of(s3[1:2, 0:T])

    def final_kv(k, zc):
        near = gathered(k, NEAR)
        zc.wait_recv()
        v = (near + zrecv[k].astype(F32)) * rcol[k]
        kvf[k] = v
        kv[k, c] = v.astype(BF16)
        return go(kv.at[k, c], kv.at[k, c], partner)

    def attention(k, own):
        load_g[k].wait()
        normed, queries, ups = [], [], []
        for h in range(QH):
            n = x[k, :, h * 128 : h * 128 + 128].astype(F32) * rcol[k]
            queries.append(n.astype(BF16))
            ups.append(g[k, :, h * 128 : h * 128 + 128])
        q = jnp.concatenate(queries, axis=0)
        up = jnp.concatenate(ups, axis=0)
        own.wait_recv()
        key, value = kv[k, 0], kv[k, 1]
        s = dot(key, q, 1, 1) * SCALE + bias[...]
        e = jnp.exp(s - jnp.max(s, axis=0, keepdims=True))
        p = e * (1.0 / jnp.sum(e, axis=0, keepdims=True))
        pl_low = p.astype(BF16)
        dp = dot(value, up, 1, 1)
        ds = p * (dp - jnp.sum(p * dp, axis=0, keepdims=True))
        ds_low = ds.astype(BF16)
        dkv[k, 0] = dot(ds_low, q, 1, 0) * SCALE
        dkv[k, 1] = dot(pl_low, up, 1, 0)
        pair = go(dkv.at[k, 1 - c], dkvr.at[k], partner)
        dqs = dot(ds_low, key, 0, 0) * SCALE
        att = dot(pl_low, value, 0, 0)
        inner = jnp.zeros((T, 128), F32)
        for h in range(QH):
            cols = slice(h * 128, h * 128 + 128)
            rows = slice(h * T, h * T + T)
            xf = x[k, :, cols].astype(F32)
            out[k, :, cols] = (xf + att[rows]).astype(BF16)
            dq[k, h] = dqs[rows]
            inner = inner + dqs[rows] * (xf * rcol[k])
        pair.wait_recv()
        total = dkv[k, c] + dkvr[k]
        low = total.astype(BF16)
        gath[k][c * 8 + head] = low
        i0[k, 0:1, 0:T] = row_of(inner + low.astype(F32) * kvf[k])

    class Gather:
        def __init__(self, k):
            self.k = k
            self.pair = {0: [], 1: []}

        def to(self, b, dev):
            ref = gath[self.k].at[b]
            return go(ref, ref, dev)

        def begin(self):
            b = c * 8 + head
            if self.k != MIRROR:
                self.z = self.to(b, zpeer)
            self.x_own = {d: self.to(b, xpeer[d]) for d in (2, 1, 3)}
            self.pair[0].append(self.to(b, partner))

        def forward_z(self):
            if self.k != MIRROR:
                self.z.wait_recv()
            b = c * 8 + xi * 2 + 1 - zi
            self.x_far = {d: self.to(b, xpeer[d]) for d in (2, 1, 3)}
            self.pair[1].append(self.to(b, partner))

        def forward_x(self, n):
            copies, z_ = (self.x_far, 1 - zi) if n else (self.x_own, zi)
            for d in (1, 3, 2):
                copies[d].wait_recv()
                b = c * 8 + ((xi + 4 - d) % 4) * 2 + z_
                self.pair[n].append(self.to(b, partner))

        def arrived(self, n):
            for copy in self.pair[n]:
                copy.wait_recv()

    def section_send(src, dst, dev, has_to, has_from):
        copy = remote(src, dst, dev)

        @pl.when(has_to)
        def _():
            copy.start()

        return (copy, has_to, has_from)

    crossing = []

    kv_up = final_kv(UP, z_up)
    i0[...] = jnp.zeros_like(i0)
    attention(UP, kv_up)
    first_part = len(sends)
    up = Gather(UP)
    up.begin()
    inner_z = [go(i0.at[UP], irz.at[UP], zpeer)]

    kv_down = final_kv(DOWN, z_down)
    attention(DOWN, kv_down)
    down = Gather(DOWN)
    down.begin()
    inner_z.append(go(i0.at[DOWN], irz.at[DOWN], zpeer))

    def inner_row(k):
        inner_z[k].wait_recv()
        i1[k] = i0[k] + irz[k]
        return {d: go(i1.at[k], irx.at[k, d], xpeer[d]) for d in (1, 2, 3)}

    def inner_pair(k, copies):
        for d in (1, 2, 3):
            copies[d].wait_recv()
        i2[k] = i1[k] + irx[k, 1] + irx[k, 2] + irx[k, 3]
        return go(i2.at[k], irp.at[k], partner)

    def part_of(k, n, blocks, total):
        rows = slice(n * 256, n * 256 + 256)
        pair = jnp.concatenate([gath[k][b] for b in blocks], axis=1)
        cols = [pl.multiple_of(b * 128, 128) for b in blocks]
        rhs = jnp.concatenate([w[k, rows, pl.ds(b, 128)] for b in cols], axis=1)
        return total + dot(pair, rhs, 1, 1)

    def grad_near(k):
        for n in range(2):
            total = jnp.concatenate([dq[k, 2 * n], dq[k, 2 * n + 1]], axis=1)
            for i in range(4):
                total = part_of(k, n, [i * 2 + zi, 8 + i * 2 + zi], total)
            gh[k, n] = total

    def grad_input(k, ip, target, dev, has_to, has_from):
        ip.wait_recv()
        mean = column_of((i2[k, 0:1, 0:T] + irp[k, 0:1, 0:T]) * (1.0 / D))
        r = rcol[k]
        for n in range(2):
            total = gh[k, n]
            for i in range(4):
                total = part_of(k, n, [i * 2 + 1 - zi, 9 + i * 2 - zi], total)
            for m in range(2):
                cols = slice(n * 256 + m * 128, n * 256 + m * 128 + 128)
                normed = x[k, :, cols].astype(F32) * r
                value = total[:, m * 128 : m * 128 + 128] - normed * mean
                gin[k, :, cols] = (g[k, :, cols].astype(F32) + r * value).astype(BF16)
            cols = slice(n * 256, n * 256 + 256)
            crossing.append(section_send(gin.at[k, :, cols], target.at[:, cols], dev, has_to, has_from))

    def hidden_rows(v, k, n):
        for h in range(QH):
            cols = slice(h * 128, h * 128 + 128)
            hidt[n, cols, :] = jnp.transpose(v[:, cols].astype(F32) * rcol[k]).astype(BF16)

    hidden_rows(x[DOWN], DOWN, 0)
    sq_m.wait_recv()
    rcol[MIRROR] = scale_of(srm[0:1, 0:T])
    early["mx"].wait_recv()
    hidden_rows(xm[...], MIRROR, 1)
    drain(first_part)
    up.forward_z()
    ix_up = inner_row(UP)
    ref = gath[UP].at[c * 8 + head]
    to_mirror = [go(ref, gath[MIRROR].at[c * 8 + head], dev) for dev in (mirror, mirror_z)]
    up.forward_x(0)
    up.arrived(0)
    grad_near(UP)
    down.forward_x(0)
    down.forward_z()
    ix_down = inner_row(DOWN)
    second_part = len(sends)
    crossing.append(section_send(out.at[UP], hu_o, before, has_before, has_after))
    crossing.append(section_send(out.at[DOWN], hd_o, after, has_after, has_before))
    down.arrived(0)
    grad_near(DOWN)
    up.forward_x(1)
    ip_up = inner_pair(UP, ix_up)
    up.arrived(1)
    far = Gather(MIRROR)
    to_mirror[0].wait_recv()
    far.begin()
    grad_input(UP, ip_up, ru_o, after, has_after, has_before)
    to_mirror[1].wait_recv()
    far.forward_z()
    down.forward_x(1)
    ip_down = inner_pair(DOWN, ix_down)
    down.arrived(1)
    grad_input(DOWN, ip_down, rd_o, before, has_before, has_after)
    drain(second_part)
    far.forward_x(0)
    far.forward_x(1)
    far.arrived(0)
    far.arrived(1)

    for ref, here in ((hu_o, sec == sections - 1), (ru_o, sec == 0), (hd_o, sec == 0), (rd_o, sec == sections - 1)):

        @pl.when(here)
        def _(ref=ref):
            ref[...] = jnp.zeros_like(ref)

    for copy, has_to, has_from in crossing:

        @pl.when(has_to)
        def _(copy=copy):
            copy.wait_send()

        @pl.when(has_from)
        def _(copy=copy):
            copy.wait_recv()

    drain(len(sends))
    assert used[0] == COPIES and used[1] == LOADS and used[2] == SENDS, used


def exchange(sections, xd, xu, gd, gu, wd, wu):
    act = pltpu.VMEM((T, W), BF16)
    hbm = pl.BlockSpec(memory_space=pltpu.HBM)
    vmem = pl.BlockSpec(memory_space=pltpu.VMEM)
    V = pltpu.VMEM
    small = (8, LANES)
    scratch = [
        V((2, T, W), BF16), V((2, T, W), BF16), V((2, W, 2 * HALF), BF16), V((T, W), BF16),
        V((T, QH * T), F32),
        V((2, 4, 2, T, 128), F32), V((2, 4, 2, T, 128), F32),
        V((2, 2, 4, T, 128), BF16), V((2, 2, 4, T, 128), BF16),
        V((2, 2, T, 128), F32), V((2, T, 128), BF16), V((2, T, 128), BF16),
        V((2, T, 128), F32), V((2, 2, T, 128), BF16), V((3, T, 128), F32),
        V((2, QH, T, 128), F32), V((2, 2, T, 128), F32), V((2, T, 128), F32),
        V((16, T, 128), BF16), V((2, T, W), BF16), V((2, T, W), BF16),
        V(small, F32), V(small, F32), V(small, F32), V(small, F32),
        V(small, F32), V((4,) + small, F32), V(small, F32), V(small, F32),
        V((2,) + small, F32), V((2,) + small, F32), V((2,) + small, F32),
        V((2,) + small, F32), V((2, 4) + small, F32), V((2,) + small, F32),
        pltpu.SemaphoreType.DMA((LOADS,)), pltpu.SemaphoreType.DMA((SENDS,)), pltpu.SemaphoreType.DMA((COPIES,)),
        V((2, 2, T, 256), F32),
    ]

    def kernel(*refs):
        exchange_kernel(sections, *refs)

    return pl.pallas_call(
        kernel,
        out_shape=(act, act, act, act, pltpu.VMEM((2, W, T), BF16),
                   pltpu.VMEM((2, 16, T, 128), BF16)),
        in_specs=[hbm] * 6,
        out_specs=(vmem,) * 6,
        scratch_shapes=scratch,
        name="exchange",
        compiler_params=pltpu.CompilerParams(
            collective_id=0, has_side_effects=True, vmem_limit_bytes=58 << 20),
    )(xd, xu, gd, gu, wd, wu)


def weights_kernel(hidt, gath, a, b, c, d, dw, ao, bo, co, do, stage, sems):
    copies = [pltpu.make_async_copy(src, dst, sems.at[8 + n])
              for n, (src, dst) in enumerate(((a, ao), (b, bo), (c, co), (d, do)))]
    for copy in copies:
        copy.start()
    for n in range(8):
        total = jnp.zeros((W, 256), F32)
        for m in range(2):
            pair = jnp.concatenate([gath[m, 2 * n], gath[m, 2 * n + 1]], axis=1)
            total = total + dot(hidt[m], pair, 1, 0)
        stage[n] = total
        copies.append(pltpu.make_async_copy(stage.at[n], dw.at[:, n * 256 : n * 256 + 256], sems.at[n]))
        copies[-1].start()
    for copy in copies:
        copy.wait()


def weight_sums(hidt, gath, arrays):
    act = jax.ShapeDtypeStruct((T, W), BF16)
    vmem = pl.BlockSpec(memory_space=pltpu.VMEM)
    hbm = pl.BlockSpec(memory_space=pltpu.HBM)
    return pl.pallas_call(
        weights_kernel,
        out_shape=(jax.ShapeDtypeStruct((W, 2 * HALF), F32),) + (act,) * 4,
        in_specs=[vmem] * 6,
        out_specs=(hbm,) * 5,
        scratch_shapes=[pltpu.VMEM((8, W, 256), F32), pltpu.SemaphoreType.DMA((12,))],
        name="weight_sums",
        compiler_params=pltpu.CompilerParams(vmem_limit_bytes=24 << 20),
    )(hidt, gath, *arrays)


def solution(mesh):
    sections = mesh.shape["section"]

    def on_device(xd, xu, gd, gu, wd, wu):
        *arrays, hidt, gath = exchange(sections, xd[0], xu[0], gd[0], gu[0], wd[0], wu[0])
        dw, hd, hu, rd, ru = weight_sums(hidt, gath, arrays)
        return hd[None], hu[None], rd[None], ru[None], dw[None]

    act, wts = P("section", None, "tensor"), P("section", "tensor", None)
    return jax.shard_map(
        on_device, mesh=mesh, in_specs=(act,) * 4 + (wts,) * 2,
        out_specs=(act,) * 4 + (wts,), check_vma=False)
```

```python
import jax
import jax.numpy as jnp
from jax import lax
from jax.experimental import pallas as pl
from jax.experimental.pallas import tpu as pltpu
from jax.sharding import PartitionSpec as P

MESH = pl.DeviceIdType.MESH
F32 = jnp.float32
BF16 = jnp.bfloat16

D = 8192
HEAD_DIM = 128
EPS = 1e-05
NEG_BIG = -1e30
SCALE = HEAD_DIM ** (-0.5)

T = 224
W = 512
HALF = 1024
QH = W // HEAD_DIM
LANES = 256

UP, DOWN, MIRROR = 0, 1, 2
LOADS, SENDS, COPIES = 8, 58, 95


def dot(a, b, ca, cb):
    return lax.dot_general(a, b, (((ca,), (cb,)), ((), ())), preferred_element_type=F32)


def row_of(total):
    return jnp.sum(jnp.transpose(total), axis=0, keepdims=True)


def column_of(row):
    return jnp.transpose(jnp.broadcast_to(row, (128, T)))


def exchange_kernel(sections, *refs):
    (xd_h, xu_h, gd_h, gu_h, wd_h, wu_h) = refs[:6]
    (hd_o, hu_o, rd_o, ru_o, hidt, gath_o) = refs[6:12]
    (x, g, w, xm, bias) = refs[12:17]
    (psend, precv, xsend, xrecv, acc, zsend, zrecv, kvf, kv, rcol) = refs[17:27]
    (dq, dkv, dkvr, gath_up, out, gin) = refs[27:33]
    gh = refs[50]
    (s0, s1, s2, s3, srp, srx, srz, srm) = refs[33:41]
    (i0, i1, i2, irz, irx, irp) = refs[41:47]
    (lsem, ssem, rsem) = refs[47:50]

    gath = (gath_up, gath_o.at[0], gath_o.at[1])

    sec = lax.axis_index("section")
    t = lax.axis_index("tensor")
    xi, zi, c = t // 4, (t // 2) % 2, t % 2
    mine, other = c * HALF, (1 - c) * HALF
    head = xi * 2 + zi

    def at(x_, z_, c_):
        return (sec, x_ * 4 + z_ * 2 + c_)

    partner = at(xi, zi, 1 - c)
    zpeer = at(xi, 1 - zi, c)
    xpeer = {d: at((xi + d) % 4, zi, c) for d in (1, 2, 3)}
    mirror = (sections - 1 - sec, t)
    mirror_z = (sections - 1 - sec, xi * 4 + (1 - zi) * 2 + c)
    after = (lax.rem(sec + 1, sections), t)
    before = (lax.rem(sec + sections - 1, sections), t)
    has_after = sec < sections - 1
    has_before = sec > 0

    used = [0, 0, 0]
    idle = []

    def remote(src, dst, dev, m=None):
        n = used[0]
        used[0] += 1
        if m is None:
            m = used[2]
            used[2] += 1
        return pltpu.make_async_remote_copy(
            src_ref=src, dst_ref=dst, send_sem=ssem.at[m], recv_sem=rsem.at[n],
            device_id=dev, device_id_type=MESH)

    def local(src, dst):
        n = used[1]
        used[1] += 1
        return pltpu.make_async_copy(src, dst, lsem.at[n])

    sends = []

    def go(src, dst, dev):
        if idle:
            m = idle.pop()
        else:
            m = used[2]
            used[2] += 1
        copy = remote(src, dst, dev, m)
        copy.start()
        sends.append((copy, m))
        return copy

    def drain(count):
        for copy, m in sends[:count]:
            copy.wait_send()
            idle.append(m)
        del sends[:count]

    barrier = pltpu.get_barrier_semaphore()
    for dev in (partner, zpeer, xpeer[1], xpeer[2], xpeer[3], mirror, mirror_z):
        pl.semaphore_signal(barrier, inc=1, device_id=dev, device_id_type=MESH)

    @pl.when(has_after)
    def _():
        pl.semaphore_signal(barrier, inc=1, device_id=after, device_id_type=MESH)

    @pl.when(has_before)
    def _():
        pl.semaphore_signal(barrier, inc=1, device_id=before, device_id_type=MESH)

    load_x = [local(xu_h, x.at[UP]), local(xd_h, x.at[DOWN])]
    load_g = [local(gu_h, g.at[UP]), local(gd_h, g.at[DOWN])]
    mcols, ocols = pl.ds(pl.multiple_of(mine, HALF), HALF), pl.ds(pl.multiple_of(other, HALF), HALF)
    wh = (wu_h, wd_h)
    load_wo = [local(wh[k].at[:, ocols], w.at[k, :, ocols]) for k in (UP, DOWN)]
    load_wm = [local(wh[k].at[:, mcols], w.at[k, :, mcols]) for k in (UP, DOWN)]
    load_x[UP].start()
    load_x[DOWN].start()
    load_wo[UP].start()
    load_wm[UP].start()
    load_wo[DOWN].start()
    load_wm[DOWN].start()
    load_g[UP].start()
    load_g[DOWN].start()

    FAR, NEAR = 0, 1
    PAIRS = ((2, 1), (3, 0))

    def block(k, base, side, ds):
        z_ = 1 - zi if side == FAR else zi
        cols = [pl.multiple_of(base + ((xi + d) % 4) * 256 + z_ * 128, 128) for d in ds]
        return dot(x[k], jnp.concatenate([w[k, :, pl.ds(n, 128)] for n in cols], axis=1), 1, 0)

    def squares(k):
        v = x[k].astype(F32)
        v = v * v
        total = v[:, 0:128] + v[:, 128:256] + v[:, 256:384] + v[:, 384:512]
        s0[k : k + 1, 0:T] = row_of(total)

    def for_partner(k, side, first=lambda: None):
        copies = []
        for n, ds in enumerate(PAIRS):
            v = block(k, other, side, ds)
            m = side * 2 + n
            psend[k, m, 0] = v[:, :128]
            psend[k, m, 1] = v[:, 128:]
            if n == 0:
                first()
            copies.append(go(psend.at[k, m], precv.at[k, m], partner))
        return copies

    def for_row(k, side, from_partner, first=lambda: None):
        first()
        for n, ds in enumerate(PAIRS):
            v = block(k, mine, side, ds)
            from_partner[n].wait_recv()
            for i, d in enumerate(ds):
                part = v[:, i * 128 : i * 128 + 128] + precv[k, side * 2 + n, i]
                if d == 0:
                    acc[k, side] = part
                else:
                    xsend[k, side, d] = part.astype(BF16)
        return (2, 1, 3)

    def send_row(k, side, ds):
        return {d: go(xsend.at[k, side, d], xrecv.at[k, side, d], xpeer[d]) for d in ds}

    s0[...] = jnp.zeros_like(s0)
    early = {}

    def after_entry():
        count = 7 + has_after.astype(jnp.int32) + has_before.astype(jnp.int32)
        pl.semaphore_wait(barrier, count)
        early["mx"] = go(x.at[UP], xm, mirror)
        early["sq"] = go(s0, srp, partner)

    def spread_squares():
        early["sq"].wait_recv()
        s1[...] = s0[...] + srp[...]
        early["sq_x"] = {d: go(s1, srx.at[d], xpeer[d]) for d in (1, 2, 3)}

    load_x[UP].wait()
    squares(UP)
    load_x[DOWN].wait()
    squares(DOWN)
    pair, held, row = {}, {}, {}
    load_wo[UP].wait()
    pair[UP, FAR] = for_partner(UP, FAR, after_entry)
    load_wm[UP].wait()
    row[UP, FAR] = send_row(UP, FAR, for_row(UP, FAR, pair[UP, FAR], spread_squares))
    load_wo[DOWN].wait()
    pair[DOWN, FAR] = for_partner(DOWN, FAR)
    pair[UP, NEAR] = for_partner(UP, NEAR)
    load_wm[DOWN].wait()
    held[DOWN, FAR] = for_row(DOWN, FAR, pair[DOWN, FAR])
    row[DOWN, FAR] = send_row(DOWN, FAR, held[DOWN, FAR])
    pair[DOWN, NEAR] = for_partner(DOWN, NEAR)
    held[UP, NEAR] = for_row(UP, NEAR, pair[UP, NEAR])
    sq_x = early["sq_x"]
    for d in (1, 2, 3):
        sq_x[d].wait_recv()
    s2[...] = s1[...] + srx[1] + srx[2] + srx[3]
    sq_z = go(s2, srz, zpeer)
    held[DOWN, NEAR] = for_row(DOWN, NEAR, pair[DOWN, NEAR])

    kk = lax.broadcasted_iota(jnp.int32, (T, QH * T), 0)
    qq = lax.broadcasted_iota(jnp.int32, (T, QH * T), 1)
    for h in range(QH - 1):
        qq = jnp.where(qq >= T, qq - T, qq)
    bias[...] = jnp.where(kk <= qq, 0.0, NEG_BIG)

    def gathered(k, side):
        for d in (1, 3, 2):
            row[k, side][d].wait_recv()
        parts = [xrecv[k, side, d].astype(F32) for d in (1, 3, 2)]
        return acc[k, side] + parts[0] + parts[1] + parts[2]

    def for_z(k):
        zsend[k] = gathered(k, FAR).astype(BF16)
        return go(zsend.at[k], zrecv.at[k], zpeer)

    z_up = for_z(UP)
    row[UP, NEAR] = send_row(UP, NEAR, held[UP, NEAR])
    z_down = for_z(DOWN)
    row[DOWN, NEAR] = send_row(DOWN, NEAR, held[DOWN, NEAR])
    sq_z.wait_recv()
    s3[...] = s2[...] + srz[...]
    sq_m = go(s3, srm, mirror)

    def scale_of(row):
        return column_of(lax.rsqrt(row / D + EPS))

    rcol[UP] = scale_of(s3[0:1, 0:T])
    rcol[DOWN] = scale_of(s3[1:2, 0:T])

    def final_kv(k, zc):
        near = gathered(k, NEAR)
        zc.wait_recv()
        v = (near + zrecv[k].astype(F32)) * rcol[k]
        kvf[k] = v
        kv[k, c] = v.astype(BF16)
        return go(kv.at[k, c], kv.at[k, c], partner)

    def attention(k, own):
        load_g[k].wait()
        normed, queries, ups = [], [], []
        for h in range(QH):
            n = x[k, :, h * 128 : h * 128 + 128].astype(F32) * rcol[k]
            queries.append(n.astype(BF16))
            ups.append(g[k, :, h * 128 : h * 128 + 128])
        q = jnp.concatenate(queries, axis=0)
        up = jnp.concatenate(ups, axis=0)
        own.wait_recv()
        key, value = kv[k, 0], kv[k, 1]
        s = dot(key, q, 1, 1) * SCALE + bias[...]
        e = jnp.exp(s - jnp.max(s, axis=0, keepdims=True))
        p = e * (1.0 / jnp.sum(e, axis=0, keepdims=True))
        pl_low = p.astype(BF16)
        dp = dot(value, up, 1, 1)
        ds = p * (dp - jnp.sum(p * dp, axis=0, keepdims=True))
        ds_low = ds.astype(BF16)
        dkv[k, 0] = dot(ds_low, q, 1, 0) * SCALE
        dkv[k, 1] = dot(pl_low, up, 1, 0)
        pair = go(dkv.at[k, 1 - c], dkvr.at[k], partner)
        dqs = dot(ds_low, key, 0, 0) * SCALE
        att = dot(pl_low, value, 0, 0)
        inner = jnp.zeros((T, 128), F32)
        for h in range(QH):
            cols = slice(h * 128, h * 128 + 128)
            rows = slice(h * T, h * T + T)
            xf = x[k, :, cols].astype(F32)
            out[k, :, cols] = (xf + att[rows]).astype(BF16)
            dq[k, h] = dqs[rows]
            inner = inner + dqs[rows] * (xf * rcol[k])
        pair.wait_recv()
        total = dkv[k, c] + dkvr[k]
        low = total.astype(BF16)
        gath[k][c * 8 + head] = low
        i0[k, 0:1, 0:T] = row_of(inner + low.astype(F32) * kvf[k])

    class Gather:
        def __init__(self, k):
            self.k = k
            self.pair = {0: [], 1: []}

        def to(self, b, dev):
            ref = gath[self.k].at[b]
            return go(ref, ref, dev)

        def begin(self):
            b = c * 8 + head
            if self.k != MIRROR:
                self.z = self.to(b, zpeer)
            self.x_own = {d: self.to(b, xpeer[d]) for d in (2, 1, 3)}
            self.pair[0].append(self.to(b, partner))

        def forward_z(self):
            if self.k != MIRROR:
                self.z.wait_recv()
            b = c * 8 + xi * 2 + 1 - zi
            self.x_far = {d: self.to(b, xpeer[d]) for d in (2, 1, 3)}
            self.pair[1].append(self.to(b, partner))

        def forward_x(self, n):
            copies, z_ = (self.x_far, 1 - zi) if n else (self.x_own, zi)
            for d in (1, 3, 2):
                copies[d].wait_recv()
                b = c * 8 + ((xi + 4 - d) % 4) * 2 + z_
                self.pair[n].append(self.to(b, partner))

        def arrived(self, n):
            for copy in self.pair[n]:
                copy.wait_recv()

    def section_send(src, dst, dev, has_to, has_from):
        copy = remote(src, dst, dev)

        @pl.when(has_to)
        def _():
            copy.start()

        return (copy, has_to, has_from)

    crossing = []

    kv_up = final_kv(UP, z_up)
    i0[...] = jnp.zeros_like(i0)
    attention(UP, kv_up)
    first_part = len(sends)
    up = Gather(UP)
    up.begin()
    inner_z = [go(i0.at[UP], irz.at[UP], zpeer)]

    kv_down = final_kv(DOWN, z_down)
    attention(DOWN, kv_down)
    down = Gather(DOWN)
    down.begin()
    inner_z.append(go(i0.at[DOWN], irz.at[DOWN], zpeer))

    def inner_row(k):
        inner_z[k].wait_recv()
        i1[k] = i0[k] + irz[k]
        return {d: go(i1.at[k], irx.at[k, d], xpeer[d]) for d in (1, 2, 3)}

    def inner_pair(k, copies):
        for d in (1, 2, 3):
            copies[d].wait_recv()
        i2[k] = i1[k] + irx[k, 1] + irx[k, 2] + irx[k, 3]
        return go(i2.at[k], irp.at[k], partner)

    def part_of(k, n, blocks, total):
        rows = slice(n * 256, n * 256 + 256)
        pair = jnp.concatenate([gath[k][b] for b in blocks], axis=1)
        cols = [pl.multiple_of(b * 128, 128) for b in blocks]
        rhs = jnp.concatenate([w[k, rows, pl.ds(b, 128)] for b in cols], axis=1)
        return total + dot(pair, rhs, 1, 1)

    def grad_near(k):
        for n in range(2):
            total = jnp.concatenate([dq[k, 2 * n], dq[k, 2 * n + 1]], axis=1)
            for i in range(4):
                total = part_of(k, n, [i * 2 + zi, 8 + i * 2 + zi], total)
            gh[k, n] = total

    def grad_input(k, ip, target, dev, has_to, has_from):
        ip.wait_recv()
        mean = column_of((i2[k, 0:1, 0:T] + irp[k, 0:1, 0:T]) * (1.0 / D))
        r = rcol[k]
        for n in range(2):
            total = gh[k, n]
            for i in range(4):
                total = part_of(k, n, [i * 2 + 1 - zi, 9 + i * 2 - zi], total)
            for m in range(2):
                cols = slice(n * 256 + m * 128, n * 256 + m * 128 + 128)
                normed = x[k, :, cols].astype(F32) * r
                value = total[:, m * 128 : m * 128 + 128] - normed * mean
                gin[k, :, cols] = (g[k, :, cols].astype(F32) + r * value).astype(BF16)
            cols = slice(n * 256, n * 256 + 256)
            crossing.append(section_send(gin.at[k, :, cols], target.at[:, cols], dev, has_to, has_from))

    def hidden_rows(v, k, n):
        for h in range(QH):
            cols = slice(h * 128, h * 128 + 128)
            hidt[n, cols, :] = jnp.transpose(v[:, cols].astype(F32) * rcol[k]).astype(BF16)

    hidden_rows(x[DOWN], DOWN, 0)
    sq_m.wait_recv()
    rcol[MIRROR] = scale_of(srm[0:1, 0:T])
    early["mx"].wait_recv()
    hidden_rows(xm[...], MIRROR, 1)
    drain(first_part)
    up.forward_z()
    ix_up = inner_row(UP)
    up.forward_x(0)
    up.arrived(0)
    grad_near(UP)
    ref = gath[UP].at[c * 8 + head]
    to_mirror = [go(ref, gath[MIRROR].at[c * 8 + head], dev) for dev in (mirror, mirror_z)]
    down.forward_x(0)
    down.forward_z()
    ix_down = inner_row(DOWN)
    second_part = len(sends)
    crossing.append(section_send(out.at[UP], hu_o, before, has_before, has_after))
    crossing.append(section_send(out.at[DOWN], hd_o, after, has_after, has_before))
    down.arrived(0)
    grad_near(DOWN)
    up.forward_x(1)
    ip_up = inner_pair(UP, ix_up)
    up.arrived(1)
    far = Gather(MIRROR)
    to_mirror[0].wait_recv()
    far.begin()
    grad_input(UP, ip_up, ru_o, after, has_after, has_before)
    to_mirror[1].wait_recv()
    far.forward_z()
    down.forward_x(1)
    ip_down = inner_pair(DOWN, ix_down)
    down.arrived(1)
    grad_input(DOWN, ip_down, rd_o, before, has_before, has_after)
    drain(second_part)
    far.forward_x(0)
    far.forward_x(1)
    far.arrived(0)
    far.arrived(1)

    for ref, here in ((hu_o, sec == sections - 1), (ru_o, sec == 0), (hd_o, sec == 0), (rd_o, sec == sections - 1)):

        @pl.when(here)
        def _(ref=ref):
            ref[...] = jnp.zeros_like(ref)

    for copy, has_to, has_from in crossing:

        @pl.when(has_to)
        def _(copy=copy):
            copy.wait_send()

        @pl.when(has_from)
        def _(copy=copy):
            copy.wait_recv()

    drain(len(sends))
    assert used[0] == COPIES and used[1] == LOADS and used[2] == SENDS, used


def exchange(sections, xd, xu, gd, gu, wd, wu):
    act = pltpu.VMEM((T, W), BF16)
    hbm = pl.BlockSpec(memory_space=pltpu.HBM)
    vmem = pl.BlockSpec(memory_space=pltpu.VMEM)
    V = pltpu.VMEM
    small = (8, LANES)
    scratch = [
        V((2, T, W), BF16), V((2, T, W), BF16), V((2, W, 2 * HALF), BF16), V((T, W), BF16),
        V((T, QH * T), F32),
        V((2, 4, 2, T, 128), F32), V((2, 4, 2, T, 128), F32),
        V((2, 2, 4, T, 128), BF16), V((2, 2, 4, T, 128), BF16),
        V((2, 2, T, 128), F32), V((2, T, 128), BF16), V((2, T, 128), BF16),
        V((2, T, 128), F32), V((2, 2, T, 128), BF16), V((3, T, 128), F32),
        V((2, QH, T, 128), F32), V((2, 2, T, 128), F32), V((2, T, 128), F32),
        V((16, T, 128), BF16), V((2, T, W), BF16), V((2, T, W), BF16),
        V(small, F32), V(small, F32), V(small, F32), V(small, F32),
        V(small, F32), V((4,) + small, F32), V(small, F32), V(small, F32),
        V((2,) + small, F32), V((2,) + small, F32), V((2,) + small, F32),
        V((2,) + small, F32), V((2, 4) + small, F32), V((2,) + small, F32),
        pltpu.SemaphoreType.DMA((LOADS,)), pltpu.SemaphoreType.DMA((SENDS,)), pltpu.SemaphoreType.DMA((COPIES,)),
        V((2, 2, T, 256), F32),
    ]

    def kernel(*refs):
        exchange_kernel(sections, *refs)

    return pl.pallas_call(
        kernel,
        out_shape=(act, act, act, act, pltpu.VMEM((2, W, T), BF16),
                   pltpu.VMEM((2, 16, T, 128), BF16)),
        in_specs=[hbm] * 6,
        out_specs=(vmem,) * 6,
        scratch_shapes=scratch,
        name="exchange",
        compiler_params=pltpu.CompilerParams(
            collective_id=0, has_side_effects=True, vmem_limit_bytes=58 << 20),
    )(xd, xu, gd, gu, wd, wu)


def weights_kernel(hidt, gath, a, b, c, d, dw, ao, bo, co, do, stage, sems):
    copies = [pltpu.make_async_copy(src, dst, sems.at[8 + n])
              for n, (src, dst) in enumerate(((a, ao), (b, bo), (c, co), (d, do)))]
    for copy in copies:
        copy.start()
    for n in range(8):
        total = jnp.zeros((W, 256), F32)
        for m in range(2):
            pair = jnp.concatenate([gath[m, 2 * n], gath[m, 2 * n + 1]], axis=1)
            total = total + dot(hidt[m], pair, 1, 0)
        stage[n] = total
        copies.append(pltpu.make_async_copy(stage.at[n], dw.at[:, n * 256 : n * 256 + 256], sems.at[n]))
        copies[-1].start()
    for copy in copies:
        copy.wait()


def weight_sums(hidt, gath, arrays):
    act = jax.ShapeDtypeStruct((T, W), BF16)
    vmem = pl.BlockSpec(memory_space=pltpu.VMEM)
    hbm = pl.BlockSpec(memory_space=pltpu.HBM)
    return pl.pallas_call(
        weights_kernel,
        out_shape=(jax.ShapeDtypeStruct((W, 2 * HALF), F32),) + (act,) * 4,
        in_specs=[vmem] * 6,
        out_specs=(hbm,) * 5,
        scratch_shapes=[pltpu.VMEM((8, W, 256), F32), pltpu.SemaphoreType.DMA((12,))],
        name="weight_sums",
        compiler_params=pltpu.CompilerParams(vmem_limit_bytes=24 << 20),
    )(hidt, gath, *arrays)


def solution(mesh):
    sections = mesh.shape["section"]

    def on_device(xd, xu, gd, gu, wd, wu):
        *arrays, hidt, gath = exchange(sections, xd[0], xu[0], gd[0], gu[0], wd[0], wu[0])
        dw, hd, hu, rd, ru = weight_sums(hidt, gath, arrays)
        return hd[None], hu[None], rd[None], ru[None], dw[None]

    act, wts = P("section", None, "tensor"), P("section", "tensor", None)
    return jax.shard_map(
        on_device, mesh=mesh, in_specs=(act,) * 4 + (wts,) * 2,
        out_specs=(act,) * 4 + (wts,), check_vma=False)
```
